512 devices in a mesh: dp: 32 (over y, x), col: 16 (over z, core).
Axes of the slice: x: 4, y: 8, z: 8, core: 2. Of those that a mesh axis runs over, the one named last changes fastest.
Arguments:
- grad_out: bfloat16 [32768, 3584], P('dp', 'col'), may hold values from -6 to 6
- residual: bfloat16 [32768, 3584], P('dp', 'col'), may hold values from -6 to 6
- confounders: bfloat16 [32768, 512], P('dp'), may hold values from -6 to 6
- gram_factor: float32 [512, 512], replicated, as said below
- proj_weight: bfloat16 [3584, 3584], P('dp', 'col'), may hold values from -0.09375 to 0.09375
- doc_lengths: int32 [32768], P(('dp', 'col')), may hold values from 1 to 512, as said below
Outputs:
- token_grad: float32 [32768, 3584], P(('dp', 'col'))
- weight_grad: float32 [3584, 3584], P('dp', 'col')
The draws below stay inside these ranges and needn't reach their ends.
Inputs may be any that keep to these rules, and one draw needn't show every extreme that they name: `gram_factor`: lower triangular with a positive diagonal. `doc_lengths`: at least one document has 512 tokens.
All inputs are finite; a program needn't handle non-finite values.
Results may differ from the reference program's by a relative error of at most 0.0026.
Values may be sent and summed in bfloat16 or wider, within the bound.
No kernel may reach another device: no remote copies, remote signals or barrier semaphores. Data moves between devices by JAX's collectives and lax.ppermute only.
A program may use at most 64 MiB of HBM per device.

```python
import jax
import jax.numpy as jnp
from jax import lax

D = 3584
OUT = 3584
K = 512
LEN_MAX = 512
DOCS = 32768


def draw_gram_factor(key, part):
    key_diag = jax.random.fold_in(key, 11)
    key_lower = jax.random.fold_in(key, 12)
    diag_vals = jax.random.uniform(key_diag, (K,), jnp.float32, 0.35, 0.7)
    lower_vals = jax.random.normal(key_lower, (K, K), jnp.float32) * (0.15 / K ** 0.5)
    row_ids = jnp.arange(K)[:, None]
    col_ids = jnp.arange(K)[None, :]
    strict = (row_ids > col_ids).astype(jnp.float32)
    ident = (row_ids == col_ids).astype(jnp.float32)
    factor = lower_vals * strict + ident * diag_vals[:, None]
    return factor * DOCS ** 0.5


def draw_doc_lengths(key, part):
    key_expo = jax.random.fold_in(key, 21)
    key_extra = jax.random.fold_in(key, 22)
    top_expo = LEN_MAX.bit_length() - 1
    expo = jax.random.randint(key_expo, (DOCS,), 0, top_expo)
    base_len = jnp.left_shift(jnp.ones((DOCS,), jnp.int32), expo.astype(jnp.int32))
    extra = jnp.remainder(jax.random.randint(key_extra, (DOCS,), 0, 1 << 30), base_len)
    lengths = jnp.minimum(base_len + extra, LEN_MAX)
    return jnp.where(jnp.arange(DOCS) == 0, LEN_MAX, lengths).astype(jnp.int32)


def strengthened(drawn, rng, source, target, shards_of, factor):
    def block_of(axis_at):
        return (jnp.arange(drawn.shape[axis_at]) // (drawn.shape[axis_at] // shards_of)).reshape((-1,) + (1,) * (drawn.ndim - 1 - axis_at))

    one_side = jax.random.permutation(rng, shards_of)[block_of(target)]
    far = (block_of(target) + shards_of // 2) % shards_of
    return jnp.where((block_of(source) == one_side) | (block_of(source) == far), factor * drawn, drawn)


def block_scale(stream_key, extent, cuts, smallest, top_value):
    gain, own = 1.0, jax.random.fold_in(stream_key, 6)
    for axis_at, shards_of in cuts:
        heights = jnp.exp(jax.random.uniform(jax.random.fold_in(own, axis_at), (shards_of,), jnp.float32, smallest / len(cuts), top_value / len(cuts)))
        gain = gain * jnp.repeat(heights, extent[axis_at] // shards_of).reshape([-1 if axis == axis_at else 1 for axis in range(len(extent))])
    return gain


def scatter_about(key, shape, scale, bound, cuts=(), kind=jnp.bfloat16):
    drawn = scale * jax.random.normal(key, shape, jnp.float32)
    if cuts:
        drawn = drawn * block_scale(key, shape, cuts, -0.22, 0.18)
    return jnp.clip(drawn, -bound, bound).astype(kind)


def noise_with(key, dims, scale, bound, cuts, heavy, kind=jnp.bfloat16):
    array = scale * jax.random.normal(key, dims, jnp.float32)
    if cuts:
        array = array * block_scale(key, dims, cuts, -0.22, 0.18)
    return jnp.clip(strengthened(array, jax.random.fold_in(key, 3), *heavy), -bound, bound).astype(kind)


def setup_inputs(seed: int = 0) -> dict:
    key_list = jax.random.split(jax.random.key(seed), 7)
    grad_out = noise_with(key_list[0], (DOCS, OUT), 1.0, 6.0, ((0, 32), (1, 16)), (0, 1, 32, 2.75))
    residual = scatter_about(key_list[1], (DOCS, D), 1.0, 6.0, ((0, 32), (1, 16)))
    confounders = scatter_about(key_list[2], (DOCS, K), 1.0, 6.0, ((0, 32),))
    gram_factor = draw_gram_factor(jax.random.fold_in(key_list[6], 71), 0)
    proj_weight = scatter_about(key_list[4], (OUT, D), D ** -0.5, 0.09375, ((0, 32), (1, 16)))
    doc_lengths = draw_doc_lengths(jax.random.fold_in(key_list[6], 71), 0)
    return dict(grad_out=grad_out, residual=residual, confounders=confounders, gram_factor=gram_factor, proj_weight=proj_weight, doc_lengths=doc_lengths)


def solve_gram(factor, rhs):
    inner = lax.linalg.triangular_solve(factor, rhs, left_side=True, lower=True)
    return lax.linalg.triangular_solve(factor, inner, left_side=True, lower=True, transpose_a=True)

def reference(grad_out, residual, confounders, gram_factor, proj_weight, doc_lengths):
    resid_grad = jnp.dot(grad_out.astype(jnp.float32), proj_weight.astype(jnp.float32), preferred_element_type=jnp.float32)
    resid_grad_b = resid_grad.astype(jnp.bfloat16)
    moments = jnp.dot(confounders.T.astype(jnp.float32), resid_grad_b.astype(jnp.float32), preferred_element_type=jnp.float32)
    coef = solve_gram(gram_factor, moments)
    coef_b = coef.astype(jnp.bfloat16)
    pooled_grad = resid_grad - jnp.dot(confounders.astype(jnp.float32), coef_b.astype(jnp.float32), preferred_element_type=jnp.float32)
    token_grad = pooled_grad / doc_lengths.astype(jnp.float32)[:, None]
    weight_grad = jnp.dot(grad_out.T.astype(jnp.float32), residual.astype(jnp.float32), preferred_element_type=jnp.float32) * DOCS ** (-0.5)
    return (token_grad, weight_grad)
```

```python
import jax
import jax.numpy as jnp
from jax import lax
from jax.experimental import pallas as pl
from jax.experimental.pallas import tpu as pltpu
from jax.sharding import Mesh, PartitionSpec as P

HI = lax.Precision.HIGHEST
F32 = jnp.float32
BF16 = jnp.bfloat16
DP = ("y", "x")
COL = ("z", "c")


def dot_hi(a, b, dims=(((1,), (0,)), ((), ()))):
    return lax.dot_general(a, b, dims, precision=HI, preferred_element_type=F32)


def gram_inverse_kernel(factor_ref, out_ref):
    size, base, half = factor_ref.shape[0], 8, factor_ref.shape[0] // 2
    count = size // base
    factor = factor_ref[...]
    block = lax.broadcasted_iota(jnp.int32, (count, base, size), 0)
    lane = lax.broadcasted_iota(jnp.int32, (count, base, size), 2)
    own = block == lane // base
    diag = jnp.sum(jnp.where(own, factor.reshape(count, base, size), 0.0), 0)
    lane = lax.broadcasted_iota(jnp.int32, (base, size), 1) % base
    picked = jnp.concatenate([jnp.where(lane == m, diag, 0.0) for m in range(base)], 0)
    rows = lax.broadcasted_iota(jnp.int32, (size, size), 0)
    cols = lax.broadcasted_iota(jnp.int32, (size, size), 1)
    same = jnp.where(rows // base == cols // base, 1.0, 0.0).astype(F32)
    entry = dot_hi(picked, same)
    lane = lane[:1]
    solved = []
    for r in range(base):
        acc = jnp.where(lane == r, 1.0, 0.0)
        for m in range(r):
            acc = acc - entry[m * base + r : m * base + r + 1] * solved[m]
        solved.append(acc / entry[r * base + r : r * base + r + 1])
    solved = jnp.concatenate(solved, 0)
    inv = jnp.where(own, solved[None], 0.0).reshape(size, size)
    tops = [inv[:half, :half], inv[half:, half:]]
    facs = [factor[:half, :half], factor[half:, half:]]
    rows, cols = rows[:half, :half], cols[:half, :half]
    step = base
    while step < half:
        pair = (rows // (2 * step) == cols // (2 * step)) & (rows % (2 * step) >= step) & (cols % (2 * step) < step)
        tops = [t - dot_hi(t, dot_hi(jnp.where(pair, f, 0.0), t)) for t, f in zip(tops, facs)]
        step *= 2
    left = -dot_hi(tops[1], dot_hi(factor[half:, :half], tops[0]))
    trans = (((0,), (0,)), ((), ()))
    out_ref[:half, :half] = dot_hi(tops[0], tops[0], trans) + dot_hi(left, left, trans)
    out_ref[half:, :half] = dot_hi(tops[1], left, trans)
    out_ref[:half, half:] = dot_hi(left, tops[1], trans)
    out_ref[half:, half:] = dot_hi(tops[1], tops[1], trans)


def gram_inverse(factor):
    return pl.pallas_call(
        gram_inverse_kernel,
        out_shape=jax.ShapeDtypeStruct(factor.shape, F32),
        compiler_params=pltpu.CompilerParams(vmem_limit_bytes=32 * 1024 * 1024),
        name="gram_inverse",
    )(factor)


def spread(x, axes, count):
    copies = jnp.broadcast_to(x[None], (count,) + x.shape)
    return lax.all_to_all(copies, axes, split_axis=0, concat_axis=0, tiled=True)


def weight_grad_kernel(place_ref, mine_ref, theirs_ref, residual_ref, *out_refs):
    core, chip = place_ref[0], place_ref[1]
    rows = out_refs[0].shape[1]
    per = mine_ref.shape[0] // rows
    for d, out_ref in enumerate(out_refs):
        target = (chip + d) % len(out_refs)
        at = pl.ds(pl.multiple_of((target % per) * rows, rows), rows)
        cols = jnp.where(target // per == core, mine_ref[at, :], theirs_ref[at, :])
        out = lax.dot_general(cols, residual_ref[...], (((1,), (1,)), ((), ())), preferred_element_type=F32)
        out_ref[0] = out.astype(BF16)


def partial_weight_grads(place, mine, theirs, residual, blocks, parts, rows):
    width, docs = residual.shape
    spec = pl.BlockSpec((width, docs), lambda i, p: (i, 0))
    return pl.pallas_call(
        weight_grad_kernel,
        out_shape=[jax.ShapeDtypeStruct((blocks, rows, width), BF16)] * parts,
        grid_spec=pltpu.PrefetchScalarGridSpec(
            num_scalar_prefetch=1,
            grid=(blocks,),
            in_specs=[spec, spec, pl.BlockSpec((width, docs), lambda i, p: (0, 0))],
            out_specs=[pl.BlockSpec((1, rows, width), lambda i, p: (i, 0, 0))] * parts,
        ),
        name="partial_weight_grads",
    )(place, mine, theirs, residual)


def shards(grad_out, residual, confounders, gram_factor, proj_weight, doc_lengths):
    ny, nx, nz, nc = (lax.axis_size(a) for a in ("y", "x", "z", "c"))
    ndp, ncol = ny * nx, nz * nc
    docs, width = grad_out.shape
    own_rows = proj_weight.shape[0]
    kdim = confounders.shape[1]
    norm_scale = (docs * ndp) ** (-0.5)
    core = lax.axis_index("c")

    mine = lax.all_gather(grad_out.T, "z", axis=0, tiled=True)
    theirs = lax.ppermute(mine, "c", [(0, 1), (1, 0)])

    cross = lax.dot_general(confounders, grad_out, (((0,), (0,)), ((), ())), preferred_element_type=F32)
    cross = lax.all_to_all(cross.reshape(ndp, kdim // ndp, width), DP, split_axis=0, concat_axis=0, tiled=True)
    cross = spread(jnp.sum(cross, 0), COL, ncol)
    cross = jnp.transpose(cross, (1, 0, 2)).reshape(kdim // ndp, ncol * width)

    weight = lax.all_gather(proj_weight[None], "y", axis=0, tiled=True)
    half = ny // 2
    weight = [lax.all_gather(w, "x", axis=1, tiled=True) for w in (weight[:half], weight[half:])]
    weight = jnp.concatenate(weight, 0).reshape(ndp * own_rows, width)
    moments = dot_hi(cross, weight.astype(F32))
    moments = spread(moments, DP, ndp).reshape(kdim, width)
    inverse = gram_inverse(gram_factor)
    coef_b = dot_hi(inverse, moments).astype(BF16)

    place = jnp.stack([core, lax.axis_index("x")]).astype(jnp.int32)
    parts = partial_weight_grads(place, mine, theirs, residual.T, nz, nx, own_rows)
    total = parts[0].astype(F32)
    for d in range(1, nx):
        total = total + lax.ppermute(parts[d], "x", [(i, (i + d) % nx) for i in range(nx)]).astype(F32)
    parts = lax.all_to_all(total.astype(BF16), "y", split_axis=0, concat_axis=0, tiled=True)
    total = parts[0].astype(F32)
    for i in range(1, ny):
        total = total + parts[i].astype(F32)
    weight_grad = total * norm_scale

    split = weight.reshape(nz, nc, width, width)
    w_mine = lax.dynamic_index_in_dim(split, core, 1, keepdims=False).reshape(nz * width, width)
    w_theirs = lax.dynamic_index_in_dim(split, 1 - core, 1, keepdims=False).reshape(nz * width, width)
    pooled = jnp.dot(mine.T, w_mine, preferred_element_type=F32)
    pooled = pooled + jnp.dot(theirs.T, w_theirs, preferred_element_type=F32)
    pooled = pooled - jnp.dot(confounders, coef_b, preferred_element_type=F32)
    doc_grad = lax.all_to_all(pooled.astype(BF16), COL, split_axis=0, concat_axis=1, tiled=True)
    token_grad = doc_grad.astype(F32) / doc_lengths.astype(F32)[:, None]
    return (token_grad, weight_grad)


def solution(mesh):
    fine = Mesh(mesh.devices.reshape(8, 4, 8, 2), ("y", "x", "z", "c"))
    placed = (P(DP, COL), P(DP, COL), P(DP, None), P(), P(DP, COL), P(DP + COL))
    return jax.shard_map(
        shards,
        mesh=fine,
        in_specs=placed,
        out_specs=(P(DP + COL, None), P(DP, COL)),
        check_vma=False,
    )
```

```python
import jax
import jax.numpy as jnp
from jax import lax
from jax.experimental import pallas as pl
from jax.experimental.pallas import tpu as pltpu
from jax.sharding import Mesh, PartitionSpec as P

HI = lax.Precision.HIGHEST
F32 = jnp.float32
BF16 = jnp.bfloat16
DP = ("y", "x")
COL = ("z", "c")


def dot_hi(a, b, dims=(((1,), (0,)), ((), ()))):
    return lax.dot_general(a, b, dims, precision=HI, preferred_element_type=F32)


def gram_inverse_kernel(factor_ref, out_ref):
    size, base, half = factor_ref.shape[0], 8, factor_ref.shape[0] // 2
    count = size // base
    factor = factor_ref[...]
    block = lax.broadcasted_iota(jnp.int32, (count, base, size), 0)
    lane = lax.broadcasted_iota(jnp.int32, (count, base, size), 2)
    own = block == lane // base
    diag = jnp.sum(jnp.where(own, factor.reshape(count, base, size), 0.0), 0)
    lane = lax.broadcasted_iota(jnp.int32, (base, size), 1) % base
    picked = jnp.concatenate([jnp.where(lane == m, diag, 0.0) for m in range(base)], 0)
    rows = lax.broadcasted_iota(jnp.int32, (size, size), 0)
    cols = lax.broadcasted_iota(jnp.int32, (size, size), 1)
    same = jnp.where(rows // base == cols // base, 1.0, 0.0).astype(F32)
    entry = dot_hi(picked, same)
    lane = lane[:1]
    solved = []
    for r in range(base):
        acc = jnp.where(lane == r, 1.0, 0.0)
        for m in range(r):
            acc = acc - entry[m * base + r : m * base + r + 1] * solved[m]
        solved.append(acc / entry[r * base + r : r * base + r + 1])
    solved = jnp.concatenate(solved, 0)
    inv = jnp.where(own, solved[None], 0.0).reshape(size, size)
    tops = [inv[:half, :half], inv[half:, half:]]
    facs = [factor[:half, :half], factor[half:, half:]]
    rows, cols = rows[:half, :half], cols[:half, :half]
    step = base
    while step < half:
        pair = (rows // (2 * step) == cols // (2 * step)) & (rows % (2 * step) >= step) & (cols % (2 * step) < step)
        tops = [t - dot_hi(t, dot_hi(jnp.where(pair, f, 0.0), t)) for t, f in zip(tops, facs)]
        step *= 2
    left = -dot_hi(tops[1], dot_hi(factor[half:, :half], tops[0]))
    trans = (((0,), (0,)), ((), ()))
    out_ref[:half, :half] = dot_hi(tops[0], tops[0], trans) + dot_hi(left, left, trans)
    out_ref[half:, :half] = dot_hi(tops[1], left, trans)
    out_ref[:half, half:] = dot_hi(left, tops[1], trans)
    out_ref[half:, half:] = dot_hi(tops[1], tops[1], trans)


def gram_inverse(factor):
    return pl.pallas_call(
        gram_inverse_kernel,
        out_shape=jax.ShapeDtypeStruct(factor.shape, F32),
        compiler_params=pltpu.CompilerParams(vmem_limit_bytes=32 * 1024 * 1024),
        name="gram_inverse",
    )(factor)


def spread(x, axes, count):
    copies = jnp.broadcast_to(x[None], (count,) + x.shape)
    return lax.all_to_all(copies, axes, split_axis=0, concat_axis=0, tiled=True)


def pack_kernel(sums_ref, rows_ref, out_ref):
    count, width = rows_ref.shape
    share = sums_ref.shape[0] // out_ref.shape[0]
    for i in range(out_ref.shape[0]):
        out_ref[i, :, width:] = jnp.zeros((out_ref.shape[1], out_ref.shape[2] - width), BF16)
        out_ref[i, :count, :width] = rows_ref[...]
        value = sums_ref[i * share : (i + 1) * share, :]
        high = value.astype(BF16)
        out_ref[i, count : count + share, :width] = high
        out_ref[i, count + share :, :width] = (value - high.astype(F32)).astype(BF16)


def pack(sums, rows, blocks):
    total = rows.shape[0] + 2 * (sums.shape[0] // blocks)
    lanes = -(-rows.shape[1] // 128) * 128
    return pl.pallas_call(
        pack_kernel, out_shape=jax.ShapeDtypeStruct((blocks, total, lanes), BF16), name="pack"
    )(sums, rows)


def unpack_kernel(packed_ref, sums_ref, rows_ref):
    count = rows_ref.shape[0] // packed_ref.shape[0]
    share, width = sums_ref.shape
    total = jnp.zeros(sums_ref.shape, F32)
    for i in range(packed_ref.shape[0]):
        rows_ref[i * count : (i + 1) * count, :] = packed_ref[i, :count, :width]
        total = total + packed_ref[i, count : count + share, :width].astype(F32)
        total = total + packed_ref[i, count + share :, :width].astype(F32)
    sums_ref[...] = total


def unpack(packed, share, width):
    blocks, total, _ = packed.shape
    return pl.pallas_call(
        unpack_kernel,
        out_shape=[
            jax.ShapeDtypeStruct((share, width), F32),
            jax.ShapeDtypeStruct((blocks * (total - 2 * share), width), BF16),
        ],
        name="unpack",
    )(packed)


def products_kernel(place_ref, mine_ref, theirs_ref, residual_ref, weight_ref, dense_ref, *out_refs):
    core, chip = place_ref[0], place_ref[1]
    rows = out_refs[0].shape[1]
    per = mine_ref.shape[0] // rows
    cols, weights = [], []
    for d in range(len(out_refs)):
        target = (chip + d) % len(out_refs)
        at = pl.ds(pl.multiple_of((target % per) * rows, rows), rows)
        cols.append(jnp.where(target // per == core, mine_ref[at, :], theirs_ref[at, :]))
        weights.append(weight_ref[target])
    cols, weights = jnp.concatenate(cols, 0), jnp.concatenate(weights, 0)
    out = lax.dot_general(cols, residual_ref[...], (((1,), (1,)), ((), ())), preferred_element_type=F32).astype(BF16)
    for d, out_ref in enumerate(out_refs):
        out_ref[0] = out[d * rows : (d + 1) * rows]
    dense = lax.dot_general(weights, cols, (((0,), (0,)), ((), ())), preferred_element_type=F32)

    @pl.when(pl.program_id(0) == 0)
    def _():
        dense_ref[...] = dense

    @pl.when(pl.program_id(0) > 0)
    def _():
        dense_ref[...] += dense


def local_products(place, mine, theirs, residual, weight, blocks, rows):
    width, docs = residual.shape
    parts = weight.shape[0]
    spec = pl.BlockSpec((width, docs), lambda i, p: (i, 0))
    whole = pl.BlockSpec((width, docs), lambda i, p: (0, 0))
    return pl.pallas_call(
        products_kernel,
        out_shape=[jax.ShapeDtypeStruct((width, docs), F32)]
        + [jax.ShapeDtypeStruct((blocks, rows, width), BF16)] * parts,
        grid_spec=pltpu.PrefetchScalarGridSpec(
            num_scalar_prefetch=1,
            grid=(blocks,),
            in_specs=[spec, spec, whole, pl.BlockSpec((parts, rows, width), lambda i, p: (0, i, 0))],
            out_specs=[whole] + [pl.BlockSpec((1, rows, width), lambda i, p: (i, 0, 0))] * parts,
        ),
        name="local_products",
    )(place, mine, theirs, residual, weight)


def shards(grad_out, residual, confounders, gram_factor, proj_weight, doc_lengths):
    ny, nx, nz, nc = (lax.axis_size(a) for a in ("y", "x", "z", "c"))
    ndp, ncol = ny * nx, nz * nc
    docs, width = grad_out.shape
    own_rows = proj_weight.shape[0]
    kdim = confounders.shape[1]
    krows = kdim // ndp
    norm_scale = (docs * ndp) ** (-0.5)
    core = lax.axis_index("c")

    mine = lax.all_gather(grad_out.T, "z", axis=0, tiled=True)
    theirs = lax.ppermute(mine, "c", [(0, 1), (1, 0)])

    cross = lax.dot_general(confounders, grad_out, (((0,), (0,)), ((), ())), preferred_element_type=F32)
    packed = lax.all_to_all(pack(cross, proj_weight, ny), "y", split_axis=0, concat_axis=0, tiled=True)
    cross, weight = unpack(packed, nx * krows, width)
    packed = pack(cross, weight, nx)
    packed = lax.all_to_all(packed, "x", split_axis=0, concat_axis=0, tiled=True)
    cross, weight = unpack(packed, krows, width)
    cross = spread(cross, COL, ncol).reshape(nz, nc, krows, nx // nc, own_rows)
    cross = jnp.transpose(cross, (2, 1, 3, 0, 4)).reshape(krows, ncol * width)
    moments = dot_hi(cross, weight.astype(F32))
    moments = spread(moments, DP, ndp).reshape(kdim, width)
    inverse = gram_inverse(gram_factor)
    coef_b = dot_hi(inverse, moments).astype(BF16)

    place = jnp.stack([core, lax.axis_index("x")]).astype(jnp.int32)
    dense, *parts = local_products(place, mine, theirs, residual.T, weight.reshape(nx, nz * own_rows, width), nz, own_rows)
    total = parts[0].astype(F32)
    for d in range(1, nx):
        total = total + lax.ppermute(parts[d], "x", [(i, (i + d) % nx) for i in range(nx)]).astype(F32)
    total = lax.psum_scatter(total, "y", scatter_dimension=0, tiled=False)
    weight_grad = total * norm_scale

    pooled = dense.T - jnp.dot(confounders, coef_b, preferred_element_type=F32)
    doc_grad = lax.all_to_all(pooled.astype(BF16), COL, split_axis=0, concat_axis=1, tiled=True)
    token_grad = doc_grad.astype(F32) / doc_lengths.astype(F32)[:, None]
    return (token_grad, weight_grad)


def solution(mesh):
    fine = Mesh(mesh.devices.reshape(8, 4, 8, 2), ("y", "x", "z", "c"))
    placed = (P(DP, COL), P(DP, COL), P(DP, None), P(), P(DP, COL), P(DP + COL))
    return jax.shard_map(
        shards,
        mesh=fine,
        in_specs=placed,
        out_specs=(P(DP + COL, None), P(DP, COL)),
        check_vma=False,
    )
```

```python
import jax
import jax.numpy as jnp
from jax import lax
from jax.experimental import pallas as pl
from jax.experimental.pallas import tpu as pltpu
from jax.sharding import Mesh, PartitionSpec as P

HI = lax.Precision.HIGHEST
F32 = jnp.float32
BF16 = jnp.bfloat16
DP = ("y", "x")
COL = ("z", "c")


def dot_hi(a, b, dims=(((1,), (0,)), ((), ()))):
    return lax.dot_general(a, b, dims, precision=HI, preferred_element_type=F32)


def gram_inverse_kernel(factor_ref, out_ref):
    size, base, half = factor_ref.shape[0], 8, factor_ref.shape[0] // 2
    count = size // base
    factor = factor_ref[...]
    block = lax.broadcasted_iota(jnp.int32, (count, base, size), 0)
    lane = lax.broadcasted_iota(jnp.int32, (count, base, size), 2)
    own = block == lane // base
    diag = jnp.sum(jnp.where(own, factor.reshape(count, base, size), 0.0), 0)
    lane = lax.broadcasted_iota(jnp.int32, (base, size), 1) % base
    picked = jnp.concatenate([jnp.where(lane == m, diag, 0.0) for m in range(base)], 0)
    rows = lax.broadcasted_iota(jnp.int32, (size, size), 0)
    cols = lax.broadcasted_iota(jnp.int32, (size, size), 1)
    same = jnp.where(rows // base == cols // base, 1.0, 0.0).astype(F32)
    entry = dot_hi(picked, same)
    lane = lane[:1]
    solved = []
    for r in range(base):
        acc = jnp.where(lane == r, 1.0, 0.0)
        for m in range(r):
            acc = acc - entry[m * base + r : m * base + r + 1] * solved[m]
        solved.append(acc / entry[r * base + r : r * base + r + 1])
    solved = jnp.concatenate(solved, 0)
    inv = jnp.where(own, solved[None], 0.0).reshape(size, size)
    tops = [inv[:half, :half], inv[half:, half:]]
    facs = [factor[:half, :half], factor[half:, half:]]
    rows, cols = rows[:half, :half], cols[:half, :half]
    step = base
    while step < half:
        pair = (rows // (2 * step) == cols // (2 * step)) & (rows % (2 * step) >= step) & (cols % (2 * step) < step)
        tops = [t - dot_hi(t, dot_hi(jnp.where(pair, f, 0.0), t)) for t, f in zip(tops, facs)]
        step *= 2
    left = -dot_hi(tops[1], dot_hi(factor[half:, :half], tops[0]))
    trans = (((0,), (0,)), ((), ()))
    out_ref[:half, :half] = dot_hi(tops[0], tops[0], trans) + dot_hi(left, left, trans)
    out_ref[half:, :half] = dot_hi(tops[1], left, trans)
    out_ref[:half, half:] = dot_hi(left, tops[1], trans)
    out_ref[half:, half:] = dot_hi(tops[1], tops[1], trans)


def gram_inverse(factor):
    return pl.pallas_call(
        gram_inverse_kernel,
        out_shape=jax.ShapeDtypeStruct(factor.shape, F32),
        compiler_params=pltpu.CompilerParams(vmem_limit_bytes=32 * 1024 * 1024),
        name="gram_inverse",
    )(factor)


def spread(x, axes, count):
    copies = jnp.broadcast_to(x[None], (count,) + x.shape)
    return lax.all_to_all(copies, axes, split_axis=0, concat_axis=0, tiled=True)


def pack_kernel(sums_ref, rows_ref, out_ref):
    count, width = rows_ref.shape
    share = sums_ref.shape[0] // out_ref.shape[0]
    for i in range(out_ref.shape[0]):
        out_ref[i, :, width:] = jnp.zeros((out_ref.shape[1], out_ref.shape[2] - width), BF16)
        out_ref[i, :count, :width] = rows_ref[...]
        value = sums_ref[i * share : (i + 1) * share, :]
        high = value.astype(BF16)
        out_ref[i, count : count + share, :width] = high
        out_ref[i, count + share :, :width] = (value - high.astype(F32)).astype(BF16)


def pack(sums, rows, blocks):
    total = rows.shape[0] + 2 * (sums.shape[0] // blocks)
    lanes = -(-rows.shape[1] // 128) * 128
    return pl.pallas_call(
        pack_kernel, out_shape=jax.ShapeDtypeStruct((blocks, total, lanes), BF16), name="pack"
    )(sums, rows)


def unpack_kernel(packed_ref, sums_ref, rows_ref):
    count = rows_ref.shape[0] // packed_ref.shape[0]
    share, width = sums_ref.shape
    total = jnp.zeros(sums_ref.shape, F32)
    for i in range(packed_ref.shape[0]):
        rows_ref[i * count : (i + 1) * count, :] = packed_ref[i, :count, :width]
        total = total + packed_ref[i, count : count + share, :width].astype(F32)
        total = total + packed_ref[i, count + share :, :width].astype(F32)
    sums_ref[...] = total


def unpack(packed, share, width):
    blocks, total, _ = packed.shape
    return pl.pallas_call(
        unpack_kernel,
        out_shape=[
            jax.ShapeDtypeStruct((share, width), F32),
            jax.ShapeDtypeStruct((blocks * (total - 2 * share), width), BF16),
        ],
        name="unpack",
    )(packed)


def select_columns(place_ref, mine_ref, theirs_ref, targets, rows):
    per = mine_ref.shape[0] // rows
    cols = []
    for target in targets:
        at = pl.ds(pl.multiple_of((target % per) * rows, rows), rows)
        cols.append(jnp.where(target // per == place_ref[0], mine_ref[at, :], theirs_ref[at, :]))
    return jnp.concatenate(cols, 0)


def weight_grad_kernel(place_ref, mine_ref, theirs_ref, residual_ref, *out_refs):
    count, rows = len(out_refs), out_refs[0].shape[1]
    targets = [(place_ref[1] + d) % count for d in range(count)]
    cols = select_columns(place_ref, mine_ref, theirs_ref, targets, rows)
    out = lax.dot_general(cols, residual_ref[...], (((1,), (1,)), ((), ())), preferred_element_type=F32).astype(BF16)
    for d, out_ref in enumerate(out_refs):
        out_ref[0] = out[d * rows : (d + 1) * rows]


def partial_weight_grads(place, mine, theirs, residual, parts, rows):
    width, docs = residual.shape
    blocks = mine.shape[0] // width
    spec = pl.BlockSpec((width, docs), lambda i, p: (i, 0))
    return pl.pallas_call(
        weight_grad_kernel,
        out_shape=[jax.ShapeDtypeStruct((blocks, rows, width), BF16)] * parts,
        grid_spec=pltpu.PrefetchScalarGridSpec(
            num_scalar_prefetch=1,
            grid=(blocks,),
            in_specs=[spec, spec, pl.BlockSpec((width, docs), lambda i, p: (0, 0))],
            out_specs=[pl.BlockSpec((1, rows, width), lambda i, p: (i, 0, 0))] * parts,
        ),
        name="partial_weight_grads",
    )(place, mine, theirs, residual)


def dense_kernel(place_ref, mine_ref, theirs_ref, weight_ref, dense_ref):
    count, rows = weight_ref.shape[:2]
    cols = select_columns(place_ref, mine_ref, theirs_ref, list(range(count)), rows)
    weights = jnp.concatenate([weight_ref[d] for d in range(count)], 0)
    dense = lax.dot_general(weights, cols, (((0,), (0,)), ((), ())), preferred_element_type=F32)

    @pl.when(pl.program_id(0) == 0)
    def _():
        dense_ref[...] = dense

    @pl.when(pl.program_id(0) > 0)
    def _():
        dense_ref[...] += dense


def dense_grad(place, mine, theirs, weight, rows):
    parts, _, width = weight.shape
    docs = mine.shape[1]
    spec = pl.BlockSpec((width, docs), lambda i, p: (i, 0))
    return pl.pallas_call(
        dense_kernel,
        out_shape=jax.ShapeDtypeStruct((width, docs), F32),
        grid_spec=pltpu.PrefetchScalarGridSpec(
            num_scalar_prefetch=1,
            grid=(mine.shape[0] // width,),
            in_specs=[spec, spec, pl.BlockSpec((parts, rows, width), lambda i, p: (0, i, 0))],
            out_specs=pl.BlockSpec((width, docs), lambda i, p: (0, 0)),
        ),
        name="dense_grad",
    )(place, mine, theirs, weight)


def sum_kernel(place_ref, *refs):
    count = refs[0].shape[0]
    parts, outs = refs[:-count], refs[-count:]
    for d, out_ref in enumerate(outs):
        at = (place_ref[2] + d) % count
        total = parts[0][at].astype(F32)
        for part in parts[1:]:
            total = total + part[at].astype(F32)
        out_ref[...] = total.astype(BF16)


def sum_parts(place, parts):
    count, rows, width = parts[0].shape
    whole = pl.BlockSpec(parts[0].shape, lambda i, p: (0, 0, 0))
    return pl.pallas_call(
        sum_kernel,
        out_shape=[jax.ShapeDtypeStruct((rows, width), BF16)] * count,
        grid_spec=pltpu.PrefetchScalarGridSpec(
            num_scalar_prefetch=1,
            grid=(1,),
            in_specs=[whole] * len(parts),
            out_specs=[pl.BlockSpec((rows, width), lambda i, p: (0, 0))] * count,
        ),
        name="sum_parts",
    )(place, *parts)


def shards(grad_out, residual, confounders, gram_factor, proj_weight, doc_lengths):
    ny, nx, nz, nc = (lax.axis_size(a) for a in ("y", "x", "z", "c"))
    ndp, ncol = ny * nx, nz * nc
    docs, width = grad_out.shape
    own_rows = proj_weight.shape[0]
    kdim = confounders.shape[1]
    krows = kdim // ndp
    norm_scale = (docs * ndp) ** (-0.5)
    core = lax.axis_index("c")

    mine = lax.all_gather(grad_out.T, "z", axis=0, tiled=True)
    theirs = lax.ppermute(mine, "c", [(0, 1), (1, 0)])

    cross = lax.dot_general(confounders, grad_out, (((0,), (0,)), ((), ())), preferred_element_type=F32)
    packed = lax.all_to_all(pack(cross, proj_weight, ny), "y", split_axis=0, concat_axis=0, tiled=True)
    cross, weight = unpack(packed, nx * krows, width)
    packed = pack(cross, weight, nx)
    packed = lax.all_to_all(packed, "x", split_axis=0, concat_axis=0, tiled=True)
    cross, weight = unpack(packed, krows, width)
    cross = spread(cross, COL, ncol).reshape(nz, nc, krows, nx // nc, own_rows)
    cross = jnp.transpose(cross, (2, 1, 3, 0, 4)).reshape(krows, ncol * width)
    moments = dot_hi(cross, weight.astype(F32))
    moments = spread(moments, DP, ndp).reshape(kdim, width)
    inverse = gram_inverse(gram_factor)
    coef_b = dot_hi(inverse, moments).astype(BF16)

    place = jnp.stack([core, lax.axis_index("x"), lax.axis_index("y")]).astype(jnp.int32)
    parts = partial_weight_grads(place, mine, theirs, residual.T, nx, own_rows)
    moved = [lax.ppermute(parts[d], "x", [(i, (i + d) % nx) for i in range(nx)]) for d in range(1, nx)]
    parts = sum_parts(place, [parts[0], *moved])
    total = parts[0].astype(F32)
    for d in (4, 3, 5, 2, 6, 1, 7):
        moved = lax.ppermute(parts[d], "y", [(i, (i + d) % ny) for i in range(ny)])
        total = total + moved.astype(F32)
    weight_grad = total * norm_scale

    dense = dense_grad(place, mine, theirs, weight.reshape(nx, nz * own_rows, width), own_rows)
    pooled = dense.T - jnp.dot(confounders, coef_b, preferred_element_type=F32)
    doc_grad = lax.all_to_all(pooled.astype(BF16), COL, split_axis=0, concat_axis=1, tiled=True)
    token_grad = doc_grad.astype(F32) / doc_lengths.astype(F32)[:, None]
    return (token_grad, weight_grad)


def solution(mesh):
    fine = Mesh(mesh.devices.reshape(8, 4, 8, 2), ("y", "x", "z", "c"))
    placed = (P(DP, COL), P(DP, COL), P(DP, None), P(), P(DP, COL), P(DP + COL))
    return jax.shard_map(
        shards,
        mesh=fine,
        in_specs=placed,
        out_specs=(P(DP + COL, None), P(DP, COL)),
        check_vma=False,
    )
```

```python
import jax
import jax.numpy as jnp
from jax import lax
from jax.experimental import pallas as pl
from jax.experimental.pallas import tpu as pltpu
from jax.sharding import Mesh, PartitionSpec as P

HI = lax.Precision.HIGHEST
F32 = jnp.float32
BF16 = jnp.bfloat16
DP = ("y", "x")
COL = ("z", "c")


def dot_hi(a, b, dims=(((1,), (0,)), ((), ()))):
    return lax.dot_general(a, b, dims, precision=HI, preferred_element_type=F32)


def gram_inverse_kernel(factor_ref, out_ref):
    size, base, half = factor_ref.shape[0], 8, factor_ref.shape[0] // 2
    count = size // base
    factor = factor_ref[...]
    block = lax.broadcasted_iota(jnp.int32, (count, base, size), 0)
    lane = lax.broadcasted_iota(jnp.int32, (count, base, size), 2)
    own = block == lane // base
    diag = jnp.sum(jnp.where(own, factor.reshape(count, base, size), 0.0), 0)
    lane = lax.broadcasted_iota(jnp.int32, (base, size), 1) % base
    picked = jnp.concatenate([jnp.where(lane == m, diag, 0.0) for m in range(base)], 0)
    rows = lax.broadcasted_iota(jnp.int32, (size, size), 0)
    cols = lax.broadcasted_iota(jnp.int32, (size, size), 1)
    same = jnp.where(rows // base == cols // base, 1.0, 0.0).astype(F32)
    entry = dot_hi(picked, same)
    lane = lane[:1]
    solved = []
    for r in range(base):
        acc = jnp.where(lane == r, 1.0, 0.0)
        for m in range(r):
            acc = acc - entry[m * base + r : m * base + r + 1] * solved[m]
        solved.append(acc / entry[r * base + r : r * base + r + 1])
    solved = jnp.concatenate(solved, 0)
    inv = jnp.where(own, solved[None], 0.0).reshape(size, size)
    tops = [inv[:half, :half], inv[half:, half:]]
    facs = [factor[:half, :half], factor[half:, half:]]
    rows, cols = rows[:half, :half], cols[:half, :half]
    step = base
    while step < half:
        pair = (rows // (2 * step) == cols // (2 * step)) & (rows % (2 * step) >= step) & (cols % (2 * step) < step)
        tops = [t - dot_hi(t, dot_hi(jnp.where(pair, f, 0.0), t)) for t, f in zip(tops, facs)]
        step *= 2
    left = -dot_hi(tops[1], dot_hi(factor[half:, :half], tops[0]))
    trans = (((0,), (0,)), ((), ()))
    out_ref[:half, :half] = dot_hi(tops[0], tops[0], trans) + dot_hi(left, left, trans)
    out_ref[half:, :half] = dot_hi(tops[1], left, trans)
    out_ref[:half, half:] = dot_hi(left, tops[1], trans)
    out_ref[half:, half:] = dot_hi(tops[1], tops[1], trans)


def gram_inverse(factor):
    return pl.pallas_call(
        gram_inverse_kernel,
        out_shape=jax.ShapeDtypeStruct(factor.shape, F32),
        compiler_params=pltpu.CompilerParams(vmem_limit_bytes=32 * 1024 * 1024),
        name="gram_inverse",
    )(factor)


def lanes(width):
    return -(-width // 128) * 128


def spread(x, axes, count):
    copies = jnp.broadcast_to(x[None], (count,) + x.shape)
    return lax.all_to_all(copies, axes, split_axis=0, concat_axis=0, tiled=True)


def select_columns(place_ref, mine_ref, theirs_ref, targets, rows):
    per = mine_ref.shape[0] // rows
    cols = []
    for target in targets:
        at = pl.ds(pl.multiple_of((target % per) * rows, rows), rows)
        cols.append(jnp.where(target // per == place_ref[0], mine_ref[at, :], theirs_ref[at, :]))
    return jnp.concatenate(cols, 0)


def weight_grad_kernel(place_ref, mine_ref, theirs_ref, residual_ref, *out_refs):
    count, rows = len(out_refs), out_refs[0].shape[1]
    targets = [(place_ref[1] + d) % count for d in range(count)]
    cols = select_columns(place_ref, mine_ref, theirs_ref, targets, rows)
    out = lax.dot_general(cols, residual_ref[...], (((1,), (0,)), ((), ())), preferred_element_type=F32).astype(BF16)
    for d, out_ref in enumerate(out_refs):
        out_ref[0] = out[d * rows : (d + 1) * rows]


def partial_weight_grads(place, mine, theirs, residual, parts, rows):
    docs, width = residual.shape
    blocks = mine.shape[0] // width
    spec = pl.BlockSpec((width, docs), lambda i, p: (i, 0))
    return pl.pallas_call(
        weight_grad_kernel,
        out_shape=[jax.ShapeDtypeStruct((blocks, rows, width), BF16)] * parts,
        grid_spec=pltpu.PrefetchScalarGridSpec(
            num_scalar_prefetch=1,
            grid=(blocks,),
            in_specs=[spec, spec, pl.BlockSpec((docs, width), lambda i, p: (0, 0))],
            out_specs=[pl.BlockSpec((1, rows, width), lambda i, p: (i, 0, 0))] * parts,
        ),
        name="partial_weight_grads",
    )(place, mine, theirs, residual)


def dense_kernel(place_ref, mine_ref, theirs_ref, weight_ref, dense_ref):
    count, rows = weight_ref.shape[:2]
    cols = select_columns(place_ref, mine_ref, theirs_ref, list(range(count)), rows)
    weights = jnp.concatenate([weight_ref[d][:, : dense_ref.shape[0]] for d in range(count)], 0)
    dense = lax.dot_general(weights, cols, (((0,), (0,)), ((), ())), preferred_element_type=F32)

    @pl.when(pl.program_id(0) == 0)
    def _():
        dense_ref[...] = dense

    @pl.when(pl.program_id(0) > 0)
    def _():
        dense_ref[...] += dense


def dense_grad(place, mine, theirs, weight, width, rows):
    parts, docs = weight.shape[0], mine.shape[1]
    spec = pl.BlockSpec((width, docs), lambda i, p: (i, 0))
    return pl.pallas_call(
        dense_kernel,
        out_shape=jax.ShapeDtypeStruct((width, docs), F32),
        grid_spec=pltpu.PrefetchScalarGridSpec(
            num_scalar_prefetch=1,
            grid=(mine.shape[0] // width,),
            in_specs=[spec, spec, pl.BlockSpec((parts, rows, weight.shape[2]), lambda i, p: (0, i, 0))],
            out_specs=pl.BlockSpec((width, docs), lambda i, p: (0, 0)),
        ),
        name="dense_grad",
    )(place, mine, theirs, weight)


def sum_kernel(*refs):
    *parts, out_ref = refs
    width = parts[0].shape[2]
    for i in range(out_ref.shape[0]):
        total = parts[0][i].astype(F32)
        for part in parts[1:]:
            total = total + part[i].astype(F32)
        out_ref[i, :, :width] = total.astype(BF16)
        out_ref[i, :, width:] = jnp.zeros((out_ref.shape[1], out_ref.shape[2] - width), BF16)


def sum_parts(parts):
    count, rows, width = parts[0].shape
    return pl.pallas_call(
        sum_kernel, out_shape=jax.ShapeDtypeStruct((count, rows, lanes(width)), BF16), name="sum_parts"
    )(*parts)


def shards(grad_out, residual, confounders, gram_factor, proj_weight, doc_lengths):
    ny, nx, nz, nc = (lax.axis_size(a) for a in ("y", "x", "z", "c"))
    ndp, ncol = ny * nx, nz * nc
    docs, width = grad_out.shape
    own_rows = proj_weight.shape[0]
    kdim = confounders.shape[1]
    krows = kdim // ndp
    norm_scale = (docs * ndp) ** (-0.5)
    core = lax.axis_index("c")

    mine = lax.all_gather(grad_out.T, "z", axis=0, tiled=True)
    theirs = lax.ppermute(mine, "c", [(0, 1), (1, 0)])

    cross = lax.dot_general(confounders, grad_out, (((0,), (0,)), ((), ())), preferred_element_type=F32)
    cross = lax.all_to_all(cross.reshape(ndp, krows, width), DP, split_axis=0, concat_axis=0, tiled=True)
    cross = jnp.sum(cross, 0)
    cross = lax.all_gather(cross, COL, axis=0, tiled=False)
    cross = cross.reshape(nz, nc, krows, nx // nc, own_rows)
    cross = jnp.transpose(cross, (2, 1, 3, 0, 4)).reshape(krows, ncol * width)

    weight = jnp.pad(proj_weight, ((0, 0), (0, lanes(width) - width)))
    weight = spread(weight, "y", ny).reshape(ny * own_rows, lanes(width))
    weight = spread(weight, "x", nx)
    moments = dot_hi(cross, weight.reshape(ndp * own_rows, lanes(width))[:, :width].astype(F32))
    moments = spread(moments, DP, ndp).reshape(kdim, width)
    inverse = gram_inverse(gram_factor)
    coef_b = dot_hi(inverse, moments).astype(BF16)

    place = jnp.stack([core, lax.axis_index("x")]).astype(jnp.int32)
    parts = partial_weight_grads(place, mine, theirs, residual, nx, own_rows)
    moved = [lax.ppermute(parts[d], "x", [(i, (i + d) % nx) for i in range(nx)]) for d in range(1, nx)]
    total = sum_parts([parts[0], *moved])
    total = lax.all_to_all(total, "y", split_axis=0, concat_axis=0, tiled=True)
    total = total[:, :, :width].astype(F32)
    weight_grad = sum((total[i] for i in range(1, ny)), total[0]) * norm_scale

    dense = dense_grad(place, mine, theirs, weight, width, own_rows)
    pooled = dense.T - jnp.dot(confounders, coef_b, preferred_element_type=F32)
    doc_grad = lax.all_to_all(pooled.astype(BF16), COL, split_axis=0, concat_axis=1, tiled=True)
    token_grad = doc_grad.astype(F32) / doc_lengths.astype(F32)[:, None]
    return (token_grad, weight_grad)


def solution(mesh):
    fine = Mesh(mesh.devices.reshape(8, 4, 8, 2), ("y", "x", "z", "c"))
    placed = (P(DP, COL), P(DP, COL), P(DP, None), P(), P(DP, COL), P(DP + COL))
    return jax.shard_map(
        shards,
        mesh=fine,
        in_specs=placed,
        out_specs=(P(DP + COL, None), P(DP, COL)),
        check_vma=False,
    )
```

```python
import jax
import jax.numpy as jnp
from jax import lax
from jax.experimental import pallas as pl
from jax.experimental.pallas import tpu as pltpu
from jax.sharding import Mesh, PartitionSpec as P

HI = lax.Precision.HIGHEST
F32 = jnp.float32
BF16 = jnp.bfloat16
DP = ("y", "x")
COL = ("z", "c")


def dot_hi(a, b, dims=(((1,), (0,)), ((), ()))):
    return lax.dot_general(a, b, dims, precision=HI, preferred_element_type=F32)


def gram_inverse_kernel(factor_ref, out_ref):
    size, base, half = factor_ref.shape[0], 8, factor_ref.shape[0] // 2
    count = size // base
    factor = factor_ref[...]
    block = lax.broadcasted_iota(jnp.int32, (count, base, size), 0)
    lane = lax.broadcasted_iota(jnp.int32, (count, base, size), 2)
    own = block == lane // base
    diag = jnp.sum(jnp.where(own, factor.reshape(count, base, size), 0.0), 0)
    lane = lax.broadcasted_iota(jnp.int32, (base, size), 1) % base
    picked = jnp.concatenate([jnp.where(lane == m, diag, 0.0) for m in range(base)], 0)
    rows = lax.broadcasted_iota(jnp.int32, (size, size), 0)
    cols = lax.broadcasted_iota(jnp.int32, (size, size), 1)
    same = jnp.where(rows // base == cols // base, 1.0, 0.0).astype(F32)
    entry = dot_hi(picked, same)
    lane = lane[:1]
    solved = []
    for r in range(base):
        acc = jnp.where(lane == r, 1.0, 0.0)
        for m in range(r):
            acc = acc - entry[m * base + r : m * base + r + 1] * solved[m]
        solved.append(acc / entry[r * base + r : r * base + r + 1])
    solved = jnp.concatenate(solved, 0)
    inv = jnp.where(own, solved[None], 0.0).reshape(size, size)
    tops = [inv[:half, :half], inv[half:, half:]]
    facs = [factor[:half, :half], factor[half:, half:]]
    rows, cols = rows[:half, :half], cols[:half, :half]
    step = base
    while step < half:
        pair = (rows // (2 * step) == cols // (2 * step)) & (rows % (2 * step) >= step) & (cols % (2 * step) < step)
        tops = [t - dot_hi(t, dot_hi(jnp.where(pair, f, 0.0), t)) for t, f in zip(tops, facs)]
        step *= 2
    left = -dot_hi(tops[1], dot_hi(factor[half:, :half], tops[0]))
    trans = (((0,), (0,)), ((), ()))
    out_ref[:half, :half] = dot_hi(tops[0], tops[0], trans) + dot_hi(left, left, trans)
    out_ref[half:, :half] = dot_hi(tops[1], left, trans)
    out_ref[:half, half:] = dot_hi(left, tops[1], trans)
    out_ref[half:, half:] = dot_hi(tops[1], tops[1], trans)


def gram_inverse(factor):
    return pl.pallas_call(
        gram_inverse_kernel,
        out_shape=jax.ShapeDtypeStruct(factor.shape, F32),
        compiler_params=pltpu.CompilerParams(vmem_limit_bytes=32 * 1024 * 1024),
        name="gram_inverse",
    )(factor)


def lanes(width):
    return -(-width // 128) * 128


def spread(x, axes, count):
    copies = jnp.broadcast_to(x[None], (count,) + x.shape)
    return lax.all_to_all(copies, axes, split_axis=0, concat_axis=0, tiled=True)


def products_kernel(place_ref, mine_ref, theirs_ref, residual_ref, weight_ref, dense_ref, *refs):
    *out_refs, done_ref = refs
    count = len(out_refs)
    blocks, rows, width = out_refs[0].shape
    core, chip = place_ref[0], place_ref[1]
    per = count // 2
    dense = None
    for k, cols_ref in enumerate((mine_ref, theirs_ref)):
        owner = core if k == 0 else 1 - core
        cols = cols_ref[...]
        out = jnp.dot(cols, residual_ref[...], preferred_element_type=F32).astype(BF16)
        for i in range(blocks):
            for j in range(per):
                at = (i * per + j) * rows
                done_ref[owner * per + j, i] = out[at : at + rows]
        weights = [
            weight_ref[owner * per + j, i * rows : (i + 1) * rows, :width] for i in range(blocks) for j in range(per)
        ]
        term = lax.dot_general(
            jnp.concatenate(weights, 0), cols, (((0,), (0,)), ((), ())), preferred_element_type=F32
        )
        dense = term if dense is None else dense + term
    for d, out_ref in enumerate(out_refs):
        out_ref[...] = done_ref[(chip + d) % count]

    @pl.when(pl.program_id(0) == 0)
    def _():
        dense_ref[...] = dense

    @pl.when(pl.program_id(0) > 0)
    def _():
        dense_ref[...] += dense


def local_products(place, mine, theirs, residual, weight, rows, blocks=2):
    docs, width = residual.shape
    parts = weight.shape[0]
    total = mine.shape[0] // width
    spec = pl.BlockSpec((blocks * width, docs), lambda i, p: (i, 0))
    return pl.pallas_call(
        products_kernel,
        out_shape=[jax.ShapeDtypeStruct((width, docs), F32)]
        + [jax.ShapeDtypeStruct((total, rows, width), BF16)] * parts,
        grid_spec=pltpu.PrefetchScalarGridSpec(
            num_scalar_prefetch=1,
            grid=(total // blocks,),
            in_specs=[
                spec,
                spec,
                pl.BlockSpec((docs, width), lambda i, p: (0, 0)),
                pl.BlockSpec((parts, blocks * rows, weight.shape[2]), lambda i, p: (0, i, 0)),
            ],
            out_specs=[pl.BlockSpec((width, docs), lambda i, p: (0, 0))]
            + [pl.BlockSpec((blocks, rows, width), lambda i, p: (i, 0, 0))] * parts,
            scratch_shapes=[pltpu.VMEM((parts, blocks, rows, width), BF16)],
        ),
        name="local_products",
    )(place, mine, theirs, residual, weight)


def sum_kernel(*refs):
    *parts, out_ref = refs
    width = parts[0].shape[2]
    for i in range(out_ref.shape[0]):
        total = parts[0][i].astype(F32)
        for part in parts[1:]:
            total = total + part[i].astype(F32)
        out_ref[i, :, :width] = total.astype(BF16)
        out_ref[i, :, width:] = jnp.zeros((out_ref.shape[1], out_ref.shape[2] - width), BF16)


def sum_parts(parts):
    count, rows, width = parts[0].shape
    return pl.pallas_call(
        sum_kernel, out_shape=jax.ShapeDtypeStruct((count, rows, lanes(width)), BF16), name="sum_parts"
    )(*parts)


def shards(grad_out, residual, confounders, gram_factor, proj_weight, doc_lengths):
    ny, nx, nz, nc = (lax.axis_size(a) for a in ("y", "x", "z", "c"))
    ndp, ncol = ny * nx, nz * nc
    docs, width = grad_out.shape
    own_rows = proj_weight.shape[0]
    kdim = confounders.shape[1]
    krows = kdim // ndp
    norm_scale = (docs * ndp) ** (-0.5)
    core = lax.axis_index("c")

    mine = lax.all_gather(grad_out.T, "z", axis=0, tiled=True)
    theirs = lax.ppermute(mine, "c", [(0, 1), (1, 0)])

    cross = lax.dot_general(confounders, grad_out, (((0,), (0,)), ((), ())), preferred_element_type=F32)
    cross = lax.all_to_all(cross.reshape(ndp, krows, width), DP, split_axis=0, concat_axis=0, tiled=True)
    cross = jnp.sum(cross, 0)
    cross = lax.all_gather(cross, COL, axis=0, tiled=False)
    cross = cross.reshape(nz, nc, krows, nx // nc, own_rows)
    cross = jnp.transpose(cross, (2, 1, 3, 0, 4)).reshape(krows, ncol * width)

    weight = jnp.pad(proj_weight, ((0, 0), (0, lanes(width) - width)))
    weight = lax.all_gather(weight, "y", axis=0, tiled=True)
    weight = spread(weight, "x", nx)
    moments = dot_hi(cross, weight.reshape(ndp * own_rows, lanes(width))[:, :width].astype(F32))
    moments = spread(moments, DP, ndp).reshape(kdim, width)
    inverse = gram_inverse(gram_factor)
    coef_b = dot_hi(inverse, moments).astype(BF16)

    place = jnp.stack([core, lax.axis_index("x")]).astype(jnp.int32)
    dense, *parts = local_products(place, mine, theirs, residual, weight, own_rows)
    moved = [lax.ppermute(parts[d], "x", [(i, (i + d) % nx) for i in range(nx)]) for d in range(1, nx)]
    total = sum_parts([parts[0], *moved])
    total = lax.all_to_all(total, "y", split_axis=0, concat_axis=0, tiled=True)
    total = total[:, :, :width].astype(F32)
    weight_grad = sum((total[i] for i in range(1, ny)), total[0]) * norm_scale

    pooled = dense.T - jnp.dot(confounders, coef_b, preferred_element_type=F32)
    doc_grad = lax.all_to_all(pooled.astype(BF16), COL, split_axis=0, concat_axis=1, tiled=True)
    token_grad = doc_grad.astype(F32) / doc_lengths.astype(F32)[:, None]
    return (token_grad, weight_grad)


def solution(mesh):
    fine = Mesh(mesh.devices.reshape(8, 4, 8, 2), ("y", "x", "z", "c"))
    placed = (P(DP, COL), P(DP, COL), P(DP, None), P(), P(DP, COL), P(DP + COL))
    return jax.shard_map(
        shards,
        mesh=fine,
        in_specs=placed,
        out_specs=(P(DP + COL, None), P(DP, COL)),
        check_vma=False,
    )
```

```python
import functools

import jax
import jax.numpy as jnp
from jax import lax
from jax.experimental import pallas as pl
from jax.experimental.pallas import tpu as pltpu
from jax.sharding import Mesh, PartitionSpec as P

HI = lax.Precision.HIGHEST
F32 = jnp.float32
BF16 = jnp.bfloat16
DP = ("y", "x")
COL = ("z", "c")


def dot_hi(a, b, dims=(((1,), (0,)), ((), ()))):
    return lax.dot_general(a, b, dims, precision=HI, preferred_element_type=F32)


def gram_inverse_kernel(factor_ref, out_ref):
    size, base, half = factor_ref.shape[0], 8, factor_ref.shape[0] // 2
    count = size // base
    factor = factor_ref[...]
    block = lax.broadcasted_iota(jnp.int32, (count, base, size), 0)
    lane = lax.broadcasted_iota(jnp.int32, (count, base, size), 2)
    own = block == lane // base
    diag = jnp.sum(jnp.where(own, factor.reshape(count, base, size), 0.0), 0)
    lane = lax.broadcasted_iota(jnp.int32, (base, size), 1) % base
    picked = jnp.concatenate([jnp.where(lane == m, diag, 0.0) for m in range(base)], 0)
    rows = lax.broadcasted_iota(jnp.int32, (size, size), 0)
    cols = lax.broadcasted_iota(jnp.int32, (size, size), 1)
    same = jnp.where(rows // base == cols // base, 1.0, 0.0).astype(F32)
    entry = dot_hi(picked, same)
    lane = lane[:1]
    solved = []
    for r in range(base):
        acc = jnp.where(lane == r, 1.0, 0.0)
        for m in range(r):
            acc = acc - entry[m * base + r : m * base + r + 1] * solved[m]
        solved.append(acc / entry[r * base + r : r * base + r + 1])
    solved = jnp.concatenate(solved, 0)
    inv = jnp.where(own, solved[None], 0.0).reshape(size, size)
    tops = [inv[:half, :half], inv[half:, half:]]
    facs = [factor[:half, :half], factor[half:, half:]]
    rows, cols = rows[:half, :half], cols[:half, :half]
    step = base
    while step < half:
        pair = (rows // (2 * step) == cols // (2 * step)) & (rows % (2 * step) >= step) & (cols % (2 * step) < step)
        tops = [t - dot_hi(t, dot_hi(jnp.where(pair, f, 0.0), t)) for t, f in zip(tops, facs)]
        step *= 2
    left = -dot_hi(tops[1], dot_hi(factor[half:, :half], tops[0]))
    trans = (((0,), (0,)), ((), ()))
    out_ref[:half, :half] = dot_hi(tops[0], tops[0], trans) + dot_hi(left, left, trans)
    out_ref[half:, :half] = dot_hi(tops[1], left, trans)
    out_ref[:half, half:] = dot_hi(left, tops[1], trans)
    out_ref[half:, half:] = dot_hi(tops[1], tops[1], trans)


def gram_inverse(factor):
    return pl.pallas_call(
        gram_inverse_kernel,
        out_shape=jax.ShapeDtypeStruct(factor.shape, F32),
        compiler_params=pltpu.CompilerParams(vmem_limit_bytes=32 * 1024 * 1024),
        name="gram_inverse",
    )(factor)


def lanes(width):
    return -(-width // 128) * 128


def spread(x, axes, count):
    copies = jnp.broadcast_to(x[None], (count,) + x.shape)
    return lax.all_to_all(copies, axes, split_axis=0, concat_axis=0, tiled=True)


def weight_grad_kernel(place_ref, mine_ref, theirs_ref, residual_ref, *refs):
    *out_refs, done_ref = refs
    count = len(out_refs)
    blocks, rows, _ = out_refs[0].shape
    core, chip = place_ref[0], place_ref[1]
    per = count // 2
    for owner, cols_ref in ((core, mine_ref), (1 - core, theirs_ref)):
        out = jnp.dot(cols_ref[...], residual_ref[...], preferred_element_type=F32).astype(BF16)
        for i in range(blocks):
            for j in range(per):
                at = (i * per + j) * rows
                done_ref[owner * per + j, i] = out[at : at + rows]
    for d, out_ref in enumerate(out_refs):
        out_ref[...] = done_ref[(chip + d) % count]


def partial_weight_grads(place, mine, theirs, residual, parts, rows, blocks=2):
    docs, width = residual.shape
    total = mine.shape[0] // width
    spec = pl.BlockSpec((blocks * width, docs), lambda i, p: (i, 0))
    return pl.pallas_call(
        weight_grad_kernel,
        out_shape=[jax.ShapeDtypeStruct((total, rows, width), BF16)] * parts,
        grid_spec=pltpu.PrefetchScalarGridSpec(
            num_scalar_prefetch=1,
            grid=(total // blocks,),
            in_specs=[spec, spec, pl.BlockSpec((docs, width), lambda i, p: (0, 0))],
            out_specs=[pl.BlockSpec((blocks, rows, width), lambda i, p: (i, 0, 0))] * parts,
            scratch_shapes=[pltpu.VMEM((parts, blocks, rows, width), BF16)],
        ),
        name="partial_weight_grads",
    )(place, mine, theirs, residual)


def dense_kernel(place_ref, mine_ref, theirs_ref, weight_ref, dense_ref, *, rows):
    width, core = dense_ref.shape[0], place_ref[0]
    per = weight_ref.shape[0] // 2
    dense = None
    for owner, cols_ref in ((core, mine_ref), (1 - core, theirs_ref)):
        weights = [
            weight_ref[owner * per + j, i * rows : (i + 1) * rows, :width]
            for i in range(weight_ref.shape[1] // rows)
            for j in range(per)
        ]
        term = lax.dot_general(
            jnp.concatenate(weights, 0), cols_ref[...], (((0,), (0,)), ((), ())), preferred_element_type=F32
        )
        dense = term if dense is None else dense + term

    @pl.when(pl.program_id(0) == 0)
    def _():
        dense_ref[...] = dense

    @pl.when(pl.program_id(0) > 0)
    def _():
        dense_ref[...] += dense


def dense_grad(place, mine, theirs, weight, width, rows, blocks=2):
    parts, docs = weight.shape[0], mine.shape[1]
    spec = pl.BlockSpec((blocks * width, docs), lambda i, p: (i, 0))
    return pl.pallas_call(
        functools.partial(dense_kernel, rows=rows),
        out_shape=jax.ShapeDtypeStruct((width, docs), F32),
        grid_spec=pltpu.PrefetchScalarGridSpec(
            num_scalar_prefetch=1,
            grid=(mine.shape[0] // (blocks * width),),
            in_specs=[spec, spec, pl.BlockSpec((parts, blocks * rows, weight.shape[2]), lambda i, p: (0, i, 0))],
            out_specs=pl.BlockSpec((width, docs), lambda i, p: (0, 0)),
        ),
        name="dense_grad",
    )(place, mine, theirs, weight)


def sum_kernel(*refs):
    *parts, out_ref = refs
    width = parts[0].shape[2]
    for i in range(out_ref.shape[0]):
        total = parts[0][i].astype(F32)
        for part in parts[1:]:
            total = total + part[i].astype(F32)
        out_ref[i, :, :width] = total.astype(BF16)
        out_ref[i, :, width:] = jnp.zeros((out_ref.shape[1], out_ref.shape[2] - width), BF16)


def sum_parts(parts):
    count, rows, width = parts[0].shape
    return pl.pallas_call(
        sum_kernel, out_shape=jax.ShapeDtypeStruct((count, rows, lanes(width)), BF16), name="sum_parts"
    )(*parts)


def shards(grad_out, residual, confounders, gram_factor, proj_weight, doc_lengths):
    ny, nx, nz, nc = (lax.axis_size(a) for a in ("y", "x", "z", "c"))
    ndp, ncol = ny * nx, nz * nc
    docs, width = grad_out.shape
    own_rows = proj_weight.shape[0]
    kdim = confounders.shape[1]
    krows = kdim // ndp
    norm_scale = (docs * ndp) ** (-0.5)
    core = lax.axis_index("c")

    mine = lax.all_gather(grad_out.T, "z", axis=0, tiled=True)
    theirs = lax.ppermute(mine, "c", [(0, 1), (1, 0)])

    cross = lax.dot_general(confounders, grad_out, (((0,), (0,)), ((), ())), preferred_element_type=F32)
    cross = lax.all_to_all(cross.reshape(ndp, krows, width), DP, split_axis=0, concat_axis=0, tiled=True)
    cross = jnp.sum(cross, 0)
    cross = lax.all_gather(cross, COL, axis=0, tiled=False)
    cross = cross.reshape(nz, nc, krows, nx // nc, own_rows)
    cross = jnp.transpose(cross, (2, 1, 3, 0, 4)).reshape(krows, ncol * width)

    weight = jnp.pad(proj_weight, ((0, 0), (0, lanes(width) - width)))
    weight = spread(weight, "y", ny).reshape(ny * own_rows, lanes(width))
    weight = spread(weight, "x", nx)
    moments = dot_hi(cross, weight.reshape(ndp * own_rows, lanes(width))[:, :width].astype(F32))
    moments = spread(moments, DP, ndp).reshape(kdim, width)
    inverse = gram_inverse(gram_factor)
    coef_b = dot_hi(inverse, moments).astype(BF16)

    place = jnp.stack([core, lax.axis_index("x")]).astype(jnp.int32)
    parts = partial_weight_grads(place, mine, theirs, residual, nx, own_rows)
    moved = [lax.ppermute(parts[d], "x", [(i, (i + d) % nx) for i in range(nx)]) for d in range(1, nx)]
    total = sum_parts([parts[0], *moved])
    total = lax.all_to_all(total, "y", split_axis=0, concat_axis=0, tiled=True)
    total = total[:, :, :width].astype(F32)
    weight_grad = sum((total[i] for i in range(1, ny)), total[0]) * norm_scale

    dense = dense_grad(place, mine, theirs, weight, width, own_rows)
    pooled = dense.T - jnp.dot(confounders, coef_b, preferred_element_type=F32)
    doc_grad = lax.all_to_all(pooled.astype(BF16), COL, split_axis=0, concat_axis=1, tiled=True)
    token_grad = doc_grad.astype(F32) / doc_lengths.astype(F32)[:, None]
    return (token_grad, weight_grad)


def solution(mesh):
    fine = Mesh(mesh.devices.reshape(8, 4, 8, 2), ("y", "x", "z", "c"))
    placed = (P(DP, COL), P(DP, COL), P(DP, None), P(), P(DP, COL), P(DP + COL))
    return jax.shard_map(
        shards,
        mesh=fine,
        in_specs=placed,
        out_specs=(P(DP + COL, None), P(DP, COL)),
        check_vma=False,
    )
```

```python
import functools

import jax
import jax.numpy as jnp
from jax import lax
from jax.experimental import pallas as pl
from jax.experimental.pallas import tpu as pltpu
from jax.sharding import Mesh, PartitionSpec as P

HI = lax.Precision.HIGHEST
F32 = jnp.float32
BF16 = jnp.bfloat16
DP = ("y", "x")
COL = ("z", "c")


def dot_hi(a, b, dims=(((1,), (0,)), ((), ()))):
    return lax.dot_general(a, b, dims, precision=HI, preferred_element_type=F32)


def gram_inverse_kernel(factor_ref, out_ref):
    size, base, half = factor_ref.shape[0], 8, factor_ref.shape[0] // 2
    count = size // base
    factor = factor_ref[...]
    block = lax.broadcasted_iota(jnp.int32, (count, base, size), 0)
    lane = lax.broadcasted_iota(jnp.int32, (count, base, size), 2)
    own = block == lane // base
    diag = jnp.sum(jnp.where(own, factor.reshape(count, base, size), 0.0), 0)
    lane = lax.broadcasted_iota(jnp.int32, (base, size), 1) % base
    picked = jnp.concatenate([jnp.where(lane == m, diag, 0.0) for m in range(base)], 0)
    rows = lax.broadcasted_iota(jnp.int32, (size, size), 0)
    cols = lax.broadcasted_iota(jnp.int32, (size, size), 1)
    same = jnp.where(rows // base == cols // base, 1.0, 0.0).astype(F32)
    entry = dot_hi(picked, same)
    lane = lane[:1]
    solved = []
    for r in range(base):
        acc = jnp.where(lane == r, 1.0, 0.0)
        for m in range(r):
            acc = acc - entry[m * base + r : m * base + r + 1] * solved[m]
        solved.append(acc / entry[r * base + r : r * base + r + 1])
    solved = jnp.concatenate(solved, 0)
    inv = jnp.where(own, solved[None], 0.0).reshape(size, size)
    tops = [inv[:half, :half], inv[half:, half:]]
    facs = [factor[:half, :half], factor[half:, half:]]
    rows, cols = rows[:half, :half], cols[:half, :half]
    step = base
    while step < half:
        pair = (rows // (2 * step) == cols // (2 * step)) & (rows % (2 * step) >= step) & (cols % (2 * step) < step)
        tops = [t - dot_hi(t, dot_hi(jnp.where(pair, f, 0.0), t)) for t, f in zip(tops, facs)]
        step *= 2
    left = -dot_hi(tops[1], dot_hi(factor[half:, :half], tops[0]))
    trans = (((0,), (0,)), ((), ()))
    out_ref[:half, :half] = dot_hi(tops[0], tops[0], trans) + dot_hi(left, left, trans)
    out_ref[half:, :half] = dot_hi(tops[1], left, trans)
    out_ref[:half, half:] = dot_hi(left, tops[1], trans)
    out_ref[half:, half:] = dot_hi(tops[1], tops[1], trans)


def gram_inverse(factor):
    return pl.pallas_call(
        gram_inverse_kernel,
        out_shape=jax.ShapeDtypeStruct(factor.shape, F32),
        compiler_params=pltpu.CompilerParams(vmem_limit_bytes=32 * 1024 * 1024),
        name="gram_inverse",
    )(factor)


def lanes(width):
    return -(-width // 128) * 128


def spread(x, axes, count):
    copies = jnp.broadcast_to(x[None], (count,) + x.shape)
    return lax.all_to_all(copies, axes, split_axis=0, concat_axis=0, tiled=True)


def weight_grad_kernel(place_ref, mine_ref, theirs_ref, residual_ref, *refs):
    *out_refs, done_ref = refs
    count = len(out_refs)
    blocks, rows, _ = out_refs[0].shape
    core, chip = place_ref[0], place_ref[1]
    per = count // 2
    for owner, cols_ref in ((core, mine_ref), (1 - core, theirs_ref)):
        out = jnp.dot(cols_ref[...], residual_ref[...], preferred_element_type=F32).astype(BF16)
        for i in range(blocks):
            for j in range(per):
                at = (i * per + j) * rows
                done_ref[owner * per + j, i] = out[at : at + rows]
    for d, out_ref in enumerate(out_refs):
        out_ref[...] = done_ref[(chip + d) % count]


def partial_weight_grads(place, mine, theirs, residual, parts, rows, blocks=2):
    docs, width = residual.shape
    total = mine.shape[0] // width
    spec = pl.BlockSpec((blocks * width, docs), lambda i, p: (i, 0))
    return pl.pallas_call(
        weight_grad_kernel,
        out_shape=[jax.ShapeDtypeStruct((total, rows, width), BF16)] * parts,
        grid_spec=pltpu.PrefetchScalarGridSpec(
            num_scalar_prefetch=1,
            grid=(total // blocks,),
            in_specs=[spec, spec, pl.BlockSpec((docs, width), lambda i, p: (0, 0))],
            out_specs=[pl.BlockSpec((blocks, rows, width), lambda i, p: (i, 0, 0))] * parts,
            scratch_shapes=[pltpu.VMEM((parts, blocks, rows, width), BF16)],
        ),
        name="partial_weight_grads",
    )(place, mine, theirs, residual)


def dense_kernel(place_ref, mine_ref, theirs_ref, weight_ref, dense_ref, *, rows):
    width, core = dense_ref.shape[0], place_ref[0]
    per = weight_ref.shape[0] // 2
    dense = None
    for owner, cols_ref in ((core, mine_ref), (1 - core, theirs_ref)):
        weights = [
            weight_ref[owner * per + j, i * rows : (i + 1) * rows, :width]
            for i in range(weight_ref.shape[1] // rows)
            for j in range(per)
        ]
        term = lax.dot_general(
            jnp.concatenate(weights, 0), cols_ref[...], (((0,), (0,)), ((), ())), preferred_element_type=F32
        )
        dense = term if dense is None else dense + term

    @pl.when(pl.program_id(0) == 0)
    def _():
        dense_ref[...] = dense

    @pl.when(pl.program_id(0) > 0)
    def _():
        dense_ref[...] += dense


def dense_grad(place, mine, theirs, weight, width, rows, blocks=2):
    parts, docs = weight.shape[0], mine.shape[1]
    spec = pl.BlockSpec((blocks * width, docs), lambda i, p: (i, 0))
    return pl.pallas_call(
        functools.partial(dense_kernel, rows=rows),
        out_shape=jax.ShapeDtypeStruct((width, docs), F32),
        grid_spec=pltpu.PrefetchScalarGridSpec(
            num_scalar_prefetch=1,
            grid=(mine.shape[0] // (blocks * width),),
            in_specs=[spec, spec, pl.BlockSpec((parts, blocks * rows, weight.shape[2]), lambda i, p: (0, i, 0))],
            out_specs=pl.BlockSpec((width, docs), lambda i, p: (0, 0)),
        ),
        name="dense_grad",
    )(place, mine, theirs, weight)


def sum_kernel(place_ref, *refs):
    count = refs[0].shape[0]
    parts, outs = refs[:-count], refs[-count:]
    for d, out_ref in enumerate(outs):
        at = (place_ref[2] + d) % count
        total = parts[0][at].astype(F32)
        for part in parts[1:]:
            total = total + part[at].astype(F32)
        out_ref[...] = total.astype(BF16)


def sum_parts(place, parts):
    count, rows, width = parts[0].shape
    whole = pl.BlockSpec(parts[0].shape, lambda i, p: (0, 0, 0))
    return pl.pallas_call(
        sum_kernel,
        out_shape=[jax.ShapeDtypeStruct((rows, width), BF16)] * count,
        grid_spec=pltpu.PrefetchScalarGridSpec(
            num_scalar_prefetch=1,
            grid=(1,),
            in_specs=[whole] * len(parts),
            out_specs=[pl.BlockSpec((rows, width), lambda i, p: (0, 0))] * count,
        ),
        name="sum_parts",
    )(place, *parts)


def shards(grad_out, residual, confounders, gram_factor, proj_weight, doc_lengths):
    ny, nx, nz, nc = (lax.axis_size(a) for a in ("y", "x", "z", "c"))
    ndp, ncol = ny * nx, nz * nc
    docs, width = grad_out.shape
    own_rows = proj_weight.shape[0]
    kdim = confounders.shape[1]
    krows = kdim // ndp
    norm_scale = (docs * ndp) ** (-0.5)
    core = lax.axis_index("c")

    mine = lax.all_gather(grad_out.T, "z", axis=0, tiled=True)
    theirs = lax.ppermute(mine, "c", [(0, 1), (1, 0)])

    cross = lax.dot_general(confounders, grad_out, (((0,), (0,)), ((), ())), preferred_element_type=F32)
    cross = lax.all_to_all(cross.reshape(ndp, krows, width), DP, split_axis=0, concat_axis=0, tiled=True)
    cross = jnp.sum(cross, 0)
    cross = lax.all_gather(cross, COL, axis=0, tiled=False)
    cross = cross.reshape(nz, nc, krows, nx // nc, own_rows)
    cross = jnp.transpose(cross, (2, 1, 3, 0, 4)).reshape(krows, ncol * width)

    weight = jnp.pad(proj_weight, ((0, 0), (0, lanes(width) - width)))
    weight = spread(weight, "y", ny).reshape(ny * own_rows, lanes(width))
    weight = spread(weight, "x", nx)
    moments = dot_hi(cross, weight.reshape(ndp * own_rows, lanes(width))[:, :width].astype(F32))
    moments = spread(moments, DP, ndp).reshape(kdim, width)
    inverse = gram_inverse(gram_factor)
    coef_b = dot_hi(inverse, moments).astype(BF16)

    place = jnp.stack([core, lax.axis_index("x"), lax.axis_index("y")]).astype(jnp.int32)
    parts = partial_weight_grads(place, mine, theirs, residual, nx, own_rows)
    moved = [lax.ppermute(parts[d], "x", [(i, (i + d) % nx) for i in range(nx)]) for d in range(1, nx)]
    parts = sum_parts(place, [parts[0], *moved])
    total = parts[0].astype(F32)
    for d in range(1, ny):
        moved = lax.ppermute(parts[d], "y", [(i, (i + d) % ny) for i in range(ny)])
        total = total + moved.astype(F32)
    weight_grad = total * norm_scale

    dense = dense_grad(place, mine, theirs, weight, width, own_rows)
    pooled = dense.T - jnp.dot(confounders, coef_b, preferred_element_type=F32)
    doc_grad = lax.all_to_all(pooled.astype(BF16), COL, split_axis=0, concat_axis=1, tiled=True)
    token_grad = doc_grad.astype(F32) / doc_lengths.astype(F32)[:, None]
    return (token_grad, weight_grad)


def solution(mesh):
    fine = Mesh(mesh.devices.reshape(8, 4, 8, 2), ("y", "x", "z", "c"))
    placed = (P(DP, COL), P(DP, COL), P(DP, None), P(), P(DP, COL), P(DP + COL))
    return jax.shard_map(
        shards,
        mesh=fine,
        in_specs=placed,
        out_specs=(P(DP + COL, None), P(DP, COL)),
        check_vma=False,
    )
```

```python
import functools

import jax
import jax.numpy as jnp
from jax import lax
from jax.experimental import pallas as pl
from jax.experimental.pallas import tpu as pltpu
from jax.sharding import Mesh, PartitionSpec as P

HI = lax.Precision.HIGHEST
F32 = jnp.float32
BF16 = jnp.bfloat16
DP = ("y", "x")
COL = ("z", "c")


def dot_hi(a, b, dims=(((1,), (0,)), ((), ()))):
    return lax.dot_general(a, b, dims, precision=HI, preferred_element_type=F32)


def gram_inverse_kernel(factor_ref, out_ref):
    size, base, half = factor_ref.shape[0], 8, factor_ref.shape[0] // 2
    count = size // base
    factor = factor_ref[...]
    block = lax.broadcasted_iota(jnp.int32, (count, base, size), 0)
    lane = lax.broadcasted_iota(jnp.int32, (count, base, size), 2)
    own = block == lane // base
    diag = jnp.sum(jnp.where(own, factor.reshape(count, base, size), 0.0), 0)
    lane = lax.broadcasted_iota(jnp.int32, (base, size), 1) % base
    picked = jnp.concatenate([jnp.where(lane == m, diag, 0.0) for m in range(base)], 0)
    rows = lax.broadcasted_iota(jnp.int32, (size, size), 0)
    cols = lax.broadcasted_iota(jnp.int32, (size, size), 1)
    same = jnp.where(rows // base == cols // base, 1.0, 0.0).astype(F32)
    entry = dot_hi(picked, same)
    lane = lane[:1]
    solved = []
    for r in range(base):
        acc = jnp.where(lane == r, 1.0, 0.0)
        for m in range(r):
            acc = acc - entry[m * base + r : m * base + r + 1] * solved[m]
        solved.append(acc / entry[r * base + r : r * base + r + 1])
    solved = jnp.concatenate(solved, 0)
    inv = jnp.where(own, solved[None], 0.0).reshape(size, size)
    tops = [inv[:half, :half], inv[half:, half:]]
    facs = [factor[:half, :half], factor[half:, half:]]
    rows, cols = rows[:half, :half], cols[:half, :half]
    step = base
    while step < half:
        pair = (rows // (2 * step) == cols // (2 * step)) & (rows % (2 * step) >= step) & (cols % (2 * step) < step)
        tops = [t - dot_hi(t, dot_hi(jnp.where(pair, f, 0.0), t)) for t, f in zip(tops, facs)]
        step *= 2
    left = -dot_hi(tops[1], dot_hi(factor[half:, :half], tops[0]))
    trans = (((0,), (0,)), ((), ()))
    out_ref[:half, :half] = dot_hi(tops[0], tops[0], trans) + dot_hi(left, left, trans)
    out_ref[half:, :half] = dot_hi(tops[1], left, trans)
    out_ref[:half, half:] = dot_hi(left, tops[1], trans)
    out_ref[half:, half:] = dot_hi(tops[1], tops[1], trans)


def gram_inverse(factor):
    return pl.pallas_call(
        gram_inverse_kernel,
        out_shape=jax.ShapeDtypeStruct(factor.shape, F32),
        compiler_params=pltpu.CompilerParams(vmem_limit_bytes=32 * 1024 * 1024),
        name="gram_inverse",
    )(factor)


def lanes(width):
    return -(-width // 128) * 128


def spread(x, axes, count):
    copies = jnp.broadcast_to(x[None], (count,) + x.shape)
    return lax.all_to_all(copies, axes, split_axis=0, concat_axis=0, tiled=True)


def weight_grad_kernel(place_ref, mine_ref, theirs_ref, residual_ref, *refs):
    *out_refs, done_ref = refs
    count = len(out_refs)
    blocks, rows, _ = out_refs[0].shape
    core, chip = place_ref[0], place_ref[1]
    per = count // 2
    for owner, cols_ref in ((core, mine_ref), (1 - core, theirs_ref)):
        out = jnp.dot(cols_ref[...], residual_ref[...], preferred_element_type=F32).astype(BF16)
        for i in range(blocks):
            for j in range(per):
                at = (i * per + j) * rows
                done_ref[owner * per + j, i] = out[at : at + rows]
    for d, out_ref in enumerate(out_refs):
        out_ref[...] = done_ref[(chip + d) % count]


def partial_weight_grads(place, mine, theirs, residual, parts, rows, blocks=2):
    docs, width = residual.shape
    total = mine.shape[0] // width
    spec = pl.BlockSpec((blocks * width, docs), lambda i, p: (i, 0))
    return pl.pallas_call(
        weight_grad_kernel,
        out_shape=[jax.ShapeDtypeStruct((total, rows, width), BF16)] * parts,
        grid_spec=pltpu.PrefetchScalarGridSpec(
            num_scalar_prefetch=1,
            grid=(total // blocks,),
            in_specs=[spec, spec, pl.BlockSpec((docs, width), lambda i, p: (0, 0))],
            out_specs=[pl.BlockSpec((blocks, rows, width), lambda i, p: (i, 0, 0))] * parts,
            scratch_shapes=[pltpu.VMEM((parts, blocks, rows, width), BF16)],
        ),
        name="partial_weight_grads",
    )(place, mine, theirs, residual)


def dense_kernel(place_ref, mine_ref, theirs_ref, weight_ref, dense_ref, *, rows):
    width, core = dense_ref.shape[0], place_ref[0]
    per = weight_ref.shape[0] // 2
    dense = None
    for owner, cols_ref in ((core, mine_ref), (1 - core, theirs_ref)):
        weights = [
            weight_ref[owner * per + j, i * rows : (i + 1) * rows, :width]
            for i in range(weight_ref.shape[1] // rows)
            for j in range(per)
        ]
        term = lax.dot_general(
            jnp.concatenate(weights, 0), cols_ref[...], (((0,), (0,)), ((), ())), preferred_element_type=F32
        )
        dense = term if dense is None else dense + term

    @pl.when(pl.program_id(0) == 0)
    def _():
        dense_ref[...] = dense

    @pl.when(pl.program_id(0) > 0)
    def _():
        dense_ref[...] += dense


def dense_grad(place, mine, theirs, weight, width, rows, blocks=2):
    parts, docs = weight.shape[0], mine.shape[1]
    spec = pl.BlockSpec((blocks * width, docs), lambda i, p: (i, 0))
    return pl.pallas_call(
        functools.partial(dense_kernel, rows=rows),
        out_shape=jax.ShapeDtypeStruct((width, docs), F32),
        grid_spec=pltpu.PrefetchScalarGridSpec(
            num_scalar_prefetch=1,
            grid=(mine.shape[0] // (blocks * width),),
            in_specs=[spec, spec, pl.BlockSpec((parts, blocks * rows, weight.shape[2]), lambda i, p: (0, i, 0))],
            out_specs=pl.BlockSpec((width, docs), lambda i, p: (0, 0)),
        ),
        name="dense_grad",
    )(place, mine, theirs, weight)


def sum_kernel(place_ref, *refs):
    *parts, keep_ref, send_ref = refs
    count, chip = parts[0].shape[0], place_ref[2]
    partner = chip + 1 - 2 * (chip % 2)
    for start, out_ref in ((chip, keep_ref), (partner, send_ref)):
        for e in range(out_ref.shape[0]):
            at = (start + 2 * e) % count
            total = parts[0][at].astype(F32)
            for part in parts[1:]:
                total = total + part[at].astype(F32)
            out_ref[e] = total


def sum_parts(place, parts):
    count, rows, width = parts[0].shape
    shape = (count // 2, rows, width)
    return pl.pallas_call(
        sum_kernel,
        out_shape=[jax.ShapeDtypeStruct(shape, F32)] * 2,
        grid_spec=pltpu.PrefetchScalarGridSpec(
            num_scalar_prefetch=1,
            grid=(1,),
            in_specs=[pl.BlockSpec(parts[0].shape, lambda i, p: (0, 0, 0))] * len(parts),
            out_specs=[pl.BlockSpec(shape, lambda i, p: (0, 0, 0))] * 2,
        ),
        name="sum_parts",
    )(place, *parts)


def pair_kernel(keep_ref, moved_ref, own_ref, *out_refs):
    own_ref[...] = keep_ref[0] + moved_ref[0]
    for e, out_ref in enumerate(out_refs, 1):
        out_ref[...] = (keep_ref[e] + moved_ref[e]).astype(BF16)


def sum_pair(keep, moved):
    count, rows, width = keep.shape
    return pl.pallas_call(
        pair_kernel,
        out_shape=[jax.ShapeDtypeStruct((rows, width), F32)]
        + [jax.ShapeDtypeStruct((rows, width), BF16)] * (count - 1),
        name="sum_pair",
    )(keep, moved)


def shards(grad_out, residual, confounders, gram_factor, proj_weight, doc_lengths):
    ny, nx, nz, nc = (lax.axis_size(a) for a in ("y", "x", "z", "c"))
    ndp, ncol = ny * nx, nz * nc
    docs, width = grad_out.shape
    own_rows = proj_weight.shape[0]
    kdim = confounders.shape[1]
    krows = kdim // ndp
    norm_scale = (docs * ndp) ** (-0.5)
    core = lax.axis_index("c")

    mine = lax.all_gather(grad_out.T, "z", axis=0, tiled=True)
    theirs = lax.ppermute(mine, "c", [(0, 1), (1, 0)])

    cross = lax.dot_general(confounders, grad_out, (((0,), (0,)), ((), ())), preferred_element_type=F32)
    cross = lax.all_to_all(cross.reshape(ndp, krows, width), DP, split_axis=0, concat_axis=0, tiled=True)
    cross = jnp.sum(cross, 0)
    cross = lax.all_gather(cross, COL, axis=0, tiled=False)
    cross = cross.reshape(nz, nc, krows, nx // nc, own_rows)
    cross = jnp.transpose(cross, (2, 1, 3, 0, 4)).reshape(krows, ncol * width)

    weight = jnp.pad(proj_weight, ((0, 0), (0, lanes(width) - width)))
    weight = spread(weight, "y", ny).reshape(ny * own_rows, lanes(width))
    weight = spread(weight, "x", nx)
    moments = dot_hi(cross, weight.reshape(ndp * own_rows, lanes(width))[:, :width].astype(F32))
    moments = spread(moments, DP, ndp).reshape(kdim, width)
    inverse = gram_inverse(gram_factor)
    coef_b = dot_hi(inverse, moments).astype(BF16)

    place = jnp.stack([core, lax.axis_index("x"), lax.axis_index("y")]).astype(jnp.int32)
    parts = partial_weight_grads(place, mine, theirs, residual, nx, own_rows)
    moved = [lax.ppermute(parts[d], "x", [(i, (i + d) % nx) for i in range(nx)]) for d in range(1, nx)]
    keep, send = sum_parts(place, [parts[0], *moved])
    moved = lax.ppermute(send, "y", [(i, i ^ 1) for i in range(ny)])
    total, *parts = sum_pair(keep, moved)
    for e, part in enumerate(parts, 1):
        moved = lax.ppermute(part, "y", [(i, (i + 2 * e) % ny) for i in range(ny)])
        total = total + moved.astype(F32)
    weight_grad = total * norm_scale

    dense = dense_grad(place, mine, theirs, weight, width, own_rows)
    pooled = dense.T - jnp.dot(confounders, coef_b, preferred_element_type=F32)
    doc_grad = lax.all_to_all(pooled.astype(BF16), COL, split_axis=0, concat_axis=1, tiled=True)
    token_grad = doc_grad.astype(F32) / doc_lengths.astype(F32)[:, None]
    return (token_grad, weight_grad)


def solution(mesh):
    fine = Mesh(mesh.devices.reshape(8, 4, 8, 2), ("y", "x", "z", "c"))
    placed = (P(DP, COL), P(DP, COL), P(DP, None), P(), P(DP, COL), P(DP + COL))
    return jax.shard_map(
        shards,
        mesh=fine,
        in_specs=placed,
        out_specs=(P(DP + COL, None), P(DP, COL)),
        check_vma=False,
    )
```
